32 devices in a mesh: design: 2 (over x), tile: 8 (over z, y), mode: 2 (over core).
Axes of the slice: x: 2, y: 2, z: 4, core: 2. Of those that a mesh axis runs over, the one named last changes fastest.
Arguments:
- forward: bfloat16 [4, 2, 4096, 4096], P(('design', 'mode'), None, 'tile'), parts along dimension 0, may hold values from -6 to 6
- adjoint_next: bfloat16 [4, 2, 4096, 4096], P(('design', 'mode'), None, 'tile'), parts along dimension 0, may hold values from -6 to 6
- phase: float32 [8192, 4096], P(('design', 'tile'), 'mode'), parts along dimension 0, may hold values from -3.140625 to 3.140625
- blocks: bfloat16 [2, 128, 4, 64, 64], P(None, 'design'), parts along dimension 1, may hold values from -0.25 to 0.25
- offsets: int32 [128, 4], P('design'), parts along dimension 0, may hold values from -2 to 2, as said below
Outputs:
- phase_next: float32 [8192, 4096], P(('design', 'tile'), 'mode'), parts along dimension 0
- forward_next: bfloat16 [4, 2, 4096, 4096], P(('design', 'mode'), None, 'tile'), parts along dimension 0
The draws below stay inside these ranges and needn't reach their ends.
There are 2 independent parts, one for each index of `design`. The reference program is written for one: setup_inputs(seed, part) draws one part's arguments, and reference() takes and returns one part's arrays. A program takes and returns all parts, laid end to end along the dimension named above; each array names one. Nothing has to cross between parts.
Inputs may be any that keep to these rules, and one draw needn't show every extreme that they name: Each row of offsets holds 4 different values, all of -2 to 2 but one; row 0 holds both -2 and 2.
All inputs are finite; a program needn't handle non-finite values.
Results may differ from the reference program's by a relative error of at most 0.02.
Values may be sent and summed in bfloat16 or wider, within the bound.
A program may use at most 256 MiB of HBM per device.

```python
import jax
import jax.numpy as jnp
from jax import lax

N = 4096
BLK = 64
RADIUS = 2
BANDS = 4
MODES = 2
NB = 64


def draw_offsets(key, part):
    missing = jax.random.randint(key, (NB,), 0, 2 * RADIUS + 1).astype(jnp.int32)
    missing = jnp.where(jnp.arange(NB, dtype=jnp.int32) == 0, RADIUS, missing)
    slots = jnp.arange(BANDS, dtype=jnp.int32)[None, :]
    return (slots + (slots >= missing[:, None]).astype(jnp.int32) - RADIUS).astype(jnp.int32)


def level_of(own_key, dims, cuts, least, largest):
    gain, own = 1.0, jax.random.fold_in(own_key, 6)
    for dim, shards_of in cuts:
        steps = jnp.exp(jax.random.uniform(jax.random.fold_in(own, dim), (shards_of,), jnp.float32, least / len(cuts), largest / len(cuts)))
        gain = gain * jnp.repeat(steps, dims[dim] // shards_of).reshape([-1 if axis == dim else 1 for axis in range(len(dims))])
    return gain


def bell_draw(rng, shape, width, bound, split=(), kind=jnp.bfloat16):
    level = level_of(rng, shape, split, -0.22, 0.18) if split else 1.0
    values = jax.random.normal(rng, shape, jnp.float32) * width * level
    return jnp.minimum(jnp.maximum(values, -bound), bound).astype(kind)


def setup_inputs(seed: int = 0, part: int = 0) -> dict:
    splits = jax.random.split(jax.random.key(seed), 6)
    part_keys = jax.random.split(jax.random.fold_in(splits[5], part), 6)
    forward = bell_draw(part_keys[0], (MODES, 2, N, N), 1.0, 6.0, ((0, 2), (2, 8)))
    adjoint_next = bell_draw(part_keys[1], (MODES, 2, N, N), 1.0, 6.0, ((0, 2), (2, 8)))
    phase = jnp.clip(jax.random.uniform(part_keys[2], (N, N), jnp.float32, -3.140625, 3.140625), -3.140625, 3.140625)
    blocks = bell_draw(part_keys[3], (2, NB, BANDS, BLK, BLK), (2 * BANDS * BLK) ** -0.5, 0.25)
    offsets = draw_offsets(jax.random.fold_in(jax.random.fold_in(splits[5], part), 71), part)
    return dict(forward=forward, adjoint_next=adjoint_next, phase=phase, blocks=blocks, offsets=offsets)


def along_columns(field_in, real_part, imag_part, index_table):
    row_count = field_in.shape[1]
    pieces = field_in.reshape(2, row_count, NB, BLK)
    picked = jnp.take(pieces, index_table, axis=2)
    real_sum = jnp.einsum("prckj,ckij->prci", picked, real_part)
    imag_sum = jnp.einsum("prckj,ckij->prci", picked, imag_part)
    result = jnp.stack([real_sum[0] - imag_sum[1], imag_sum[0] + real_sum[1]])
    return result.reshape(2, row_count, NB * BLK)


def propagate(field_in, real_part, imag_part, index_table):
    middle = along_columns(field_in.astype(jnp.float32), real_part, imag_part, index_table).astype(jnp.bfloat16)
    turned = jnp.swapaxes(middle, 1, 2).astype(jnp.float32)
    return jnp.swapaxes(along_columns(turned, real_part, imag_part, index_table), 1, 2)


def reference(forward, adjoint_next, phase, blocks, offsets):
    raw_index = jnp.arange(NB, dtype=jnp.int32)[:, None] + offsets.astype(jnp.int32)
    inside = (raw_index >= 0) & (raw_index < NB)
    index_table = jnp.clip(raw_index, 0, NB - 1).astype(jnp.int32)
    zero_block = jnp.zeros((), blocks.dtype)
    real_blocks = jnp.where(inside[:, :, None, None], blocks[0], zero_block).astype(jnp.float32)
    imag_blocks = jnp.where(inside[:, :, None, None], blocks[1], zero_block).astype(jnp.float32)
    cos_old = jnp.cos(phase)
    sin_old = jnp.sin(phase)

    def mode_terms(pair):
        field_fwd, field_adj = pair
        adjoint_here = propagate(field_adj, real_blocks, -imag_blocks, index_table).astype(jnp.bfloat16)
        adjoint_here = lax.optimization_barrier(adjoint_here).astype(jnp.float32)
        fwd_real = field_fwd[0].astype(jnp.float32)
        fwd_imag = field_fwd[1].astype(jnp.float32)
        lit_real = cos_old * fwd_real - sin_old * fwd_imag
        lit_imag = sin_old * fwd_real + cos_old * fwd_imag
        term_real = adjoint_here[0] * lit_real + adjoint_here[1] * lit_imag
        term_imag = adjoint_here[0] * lit_imag - adjoint_here[1] * lit_real
        return jnp.stack([term_real, term_imag])

    terms = lax.map(mode_terms, (forward, adjoint_next))
    intersections = jnp.sum(terms, axis=(2, 3))
    gradient = jnp.sum(intersections[:, 0, None, None] * terms[:, 1] - intersections[:, 1, None, None] * terms[:, 0], axis=0)
    phase_next = phase - gradient / (4.0 * N * MODES)
    cos_new = jnp.cos(phase_next)
    sin_new = jnp.sin(phase_next)

    def launch(field_fwd):
        fwd_real = field_fwd[0].astype(jnp.float32)
        fwd_imag = field_fwd[1].astype(jnp.float32)
        launched = jnp.stack([cos_new * fwd_real - sin_new * fwd_imag, sin_new * fwd_real + cos_new * fwd_imag]).astype(jnp.bfloat16)
        return propagate(launched, real_blocks, imag_blocks, index_table).astype(jnp.bfloat16)

    forward_next = lax.map(launch, forward)
    return phase_next, forward_next
```

```python
import functools

import jax
import jax.numpy as jnp
from jax import lax
from jax.experimental import pallas as pl
from jax.experimental.pallas import tpu as pltpu
from jax.sharding import PartitionSpec as P

BLK = 64
RADIUS = 2
EDGE = RADIUS * BLK
WIDE = 256
VMEM_LIMIT = 44 * 1024 * 1024

F32 = jnp.float32
BF16 = jnp.bfloat16


def params():
    return pltpu.CompilerParams(vmem_limit_bytes=VMEM_LIMIT)


def cost(flops, moved):
    return pl.CostEstimate(flops=int(flops), bytes_accessed=int(moved), transcendentals=0)


def sincos(x):
    turns = jnp.round(x * 0.6366197723675814)
    r = x - turns * 1.5703125
    r = r - turns * 4.837512969970703125e-4
    r = r - turns * 7.549789954891882e-8
    quadrant = turns.astype(jnp.int32)
    z = r * r
    s = r + r * z * (-1.6666654611e-1 + z * (8.3321608736e-3 + z * -1.9515295891e-4))
    c = 1.0 - 0.5 * z + z * z * (4.166664568298827e-2 + z * (-1.388731625493765e-3 + z * 2.443315711809948e-5))
    swap = (quadrant & 1) == 1
    sine = jnp.where(swap, c, s)
    cosine = jnp.where(swap, s, c)
    sine = jnp.where((quadrant & 2) == 2, -sine, sine)
    cosine = jnp.where(((quadrant + 1) & 2) == 2, -cosine, cosine)
    return sine, cosine


def dot(a, b):
    return jnp.dot(a, b, preferred_element_type=F32)


def build_kernel(pos_ref, blk_ref, out_ref, *, group, transposed):
    base = pl.program_id(0) * group
    zero = jnp.zeros((BLK, BLK), F32)
    for part in range(2):
        strips = []
        for r in range(group):
            own = [blk_ref[part, r, k].astype(F32) for k in range(blk_ref.shape[2])]
            pieces = [zero] * r
            for d in range(2 * RADIUS + 1):
                piece = zero
                for k, block in enumerate(own):
                    piece = jnp.where(pos_ref[base + r, k] == d, block, piece)
                pieces.append(piece)
            pieces += [zero] * (group - 1 - r)
            strips.append(jnp.concatenate(pieces, axis=1))
        full = jnp.concatenate(strips, axis=0)
        if transposed:
            full = full.T
        out_ref[0, part] = full.astype(BF16)


def build(blocks, pos, group, transposed):
    _, rows, bands, _, _ = blocks.shape
    tall, wide = group * BLK, (group + 2 * RADIUS) * BLK
    if transposed:
        tall, wide = wide, tall
    count = rows // group
    return pl.pallas_call(
        functools.partial(build_kernel, group=group, transposed=transposed),
        out_shape=jax.ShapeDtypeStruct((count, 2, tall, wide), BF16),
        grid_spec=pltpu.PrefetchScalarGridSpec(
            num_scalar_prefetch=1,
            grid=(count,),
            in_specs=[pl.BlockSpec((2, group, bands, BLK, BLK), lambda g, p: (0, g, 0, 0, 0))],
            out_specs=pl.BlockSpec((1, 2, tall, wide), lambda g, p: (g, 0, 0, 0)),
        ),
        compiler_params=params(),
        cost_estimate=cost(0, 16 * rows * bands * BLK * BLK),
        name="build_operator",
    )(pos, blocks)


def window_specs(rows, groups):
    last = 2 * groups - 1
    return [
        pl.BlockSpec((2, rows, 128), lambda j: (0, 0, jnp.maximum(2 * j - 1, 0))),
        pl.BlockSpec((2, rows, WIDE), lambda j: (0, 0, j)),
        pl.BlockSpec((2, rows, 128), lambda j: (0, 0, jnp.minimum(2 * j + 2, last))),
    ]


def window(left, mid, right, part):
    return jnp.concatenate([left[part], mid[part], right[part]], axis=1)


def column_product(x_re, x_im, op_ref, conj):
    op_re, op_im = op_ref[0, 0], op_ref[0, 1]
    rr, ii = dot(x_re, op_re), dot(x_im, op_im)
    ri, ir = dot(x_re, op_im), dot(x_im, op_re)
    if conj:
        return (rr + ii).astype(BF16), (ri - ir).astype(BF16)
    return (rr - ii).astype(BF16), (ri + ir).astype(BF16)


def column_kernel(left, mid, right, op_ref, out_ref, *, conj):
    out_re, out_im = column_product(
        window(left, mid, right, 0), window(left, mid, right, 1), op_ref, conj
    )
    out_ref[0] = out_re
    out_ref[1] = out_im


def column_pass(field, op, conj):
    _, rows, width = field.shape
    groups = width // WIDE
    return pl.pallas_call(
        functools.partial(column_kernel, conj=conj),
        out_shape=jax.ShapeDtypeStruct(field.shape, BF16),
        grid=(groups,),
        in_specs=window_specs(rows, groups)
        + [pl.BlockSpec((1, 2, op.shape[2], WIDE), lambda j: (j, 0, 0, 0))],
        out_specs=pl.BlockSpec((2, rows, WIDE), lambda j: (0, 0, j)),
        compiler_params=params(),
        cost_estimate=cost(8 * rows * width * op.shape[2], 12 * rows * width + 2 * op.size),
        name="column_pass",
    )(field, field, field, op)


def row_groups(top, main, bottom, row_op):
    whole_re = jnp.concatenate([top[0], main[0], bottom[0]], axis=0)
    whole_im = jnp.concatenate([top[1], main[1], bottom[1]], axis=0)
    count, _, tall, deep = row_op.shape
    for i in range(count):
        m_re = whole_re[i * tall : i * tall + deep]
        m_im = whole_im[i * tall : i * tall + deep]
        op_re, op_im = row_op[i, 0], row_op[i, 1]
        out_re = dot(op_re, m_re) - dot(op_im, m_im)
        out_im = dot(op_re, m_im) + dot(op_im, m_re)
        yield i * tall, tall, out_re, out_im


def adjoint_row_kernel(tl, tm, tr, bl, bm, br, op_ref, main, row_op, lit, terms, sums):
    x_re = jnp.concatenate([window(tl, tm, tr, 0), window(bl, bm, br, 0)], axis=0)
    x_im = jnp.concatenate([window(tl, tm, tr, 1), window(bl, bm, br, 1)], axis=0)
    halo_re, halo_im = column_product(x_re, x_im, op_ref, True)

    @pl.when(pl.program_id(0) == 0)
    def _():
        sums[...] = jnp.zeros_like(sums)

    top = (halo_re[:EDGE], halo_im[:EDGE])
    bottom = (halo_re[EDGE:], halo_im[EDGE:])
    for low, tall, cj_re, cj_im in row_groups(top, main, bottom, row_op):
        cj_re = cj_re.astype(BF16).astype(F32)
        cj_im = cj_im.astype(BF16).astype(F32)
        lit_re = lit[0, low : low + tall].astype(F32)
        lit_im = lit[1, low : low + tall].astype(F32)
        t_re = cj_re * lit_re - cj_im * lit_im
        t_im = cj_re * lit_im + cj_im * lit_re
        terms[0, low : low + tall] = t_re.astype(BF16)
        terms[1, low : low + tall] = t_im.astype(BF16)
        sums[0] += jnp.sum(t_re.reshape(tall // 8, 8, WIDE), axis=0)
        sums[1] += jnp.sum(t_im.reshape(tall // 8, 8, WIDE), axis=0)


def adjoint_rows(top, bottom, op, main, row_op, lit):
    _, rows, width = main.shape
    groups = width // WIDE
    edge = window_specs(EDGE, groups)
    tile = pl.BlockSpec((2, rows, WIDE), lambda j: (0, 0, j))
    return pl.pallas_call(
        adjoint_row_kernel,
        out_shape=(
            jax.ShapeDtypeStruct(main.shape, BF16),
            jax.ShapeDtypeStruct((2, 8, WIDE), F32),
        ),
        grid=(groups,),
        in_specs=edge
        + edge
        + [
            pl.BlockSpec((1, 2, op.shape[2], WIDE), lambda j: (j, 0, 0, 0)),
            tile,
            pl.BlockSpec(row_op.shape, lambda j: (0, 0, 0, 0)),
            tile,
        ],
        out_specs=(tile, pl.BlockSpec((2, 8, WIDE), lambda j: (0, 0, 0))),
        compiler_params=params(),
        cost_estimate=cost(12 * rows * width * op.shape[2], 16 * rows * width),
        name="adjoint_rows",
    )(top, top, top, bottom, bottom, bottom, op, main, row_op, lit)


def forward_row_kernel(top, main, bottom, row_op, out):
    for low, tall, out_re, out_im in row_groups(top, main, bottom, row_op):
        out[0, 0, low : low + tall] = out_re.astype(BF16)
        out[0, 1, low : low + tall] = out_im.astype(BF16)


def forward_rows(top, main, bottom, row_op):
    _, rows, width = main.shape
    groups = width // WIDE
    edge = pl.BlockSpec((2, EDGE, WIDE), lambda j: (0, 0, j))
    return pl.pallas_call(
        forward_row_kernel,
        out_shape=jax.ShapeDtypeStruct((1,) + main.shape, BF16),
        grid=(groups,),
        in_specs=[
            edge,
            pl.BlockSpec((2, rows, WIDE), lambda j: (0, 0, j)),
            edge,
            pl.BlockSpec(row_op.shape, lambda j: (0, 0, 0, 0)),
        ],
        out_specs=pl.BlockSpec((1, 2, rows, WIDE), lambda j: (0, 0, 0, j)),
        compiler_params=params(),
        cost_estimate=cost(8 * rows * width * row_op.shape[3], 10 * rows * width),
        name="forward_rows",
    )(top, main, bottom, row_op)


def lit_kernel(phase, fwd, lit):
    sine, cosine = sincos(phase[0])
    f_re, f_im = fwd[0, 0].astype(F32), fwd[0, 1].astype(F32)
    lit[0] = (cosine * f_re - sine * f_im).astype(BF16)
    lit[1] = (sine * f_re + cosine * f_im).astype(BF16)


def light(phases, forward):
    _, _, rows, width = forward.shape
    half = phases.shape[2] // WIDE
    return pl.pallas_call(
        lit_kernel,
        out_shape=jax.ShapeDtypeStruct(forward.shape[1:], BF16),
        grid=(width // WIDE,),
        in_specs=[
            pl.BlockSpec((1, rows, WIDE), lambda j: (j // half, 0, j % half)),
            pl.BlockSpec((1, 2, rows, WIDE), lambda j: (0, 0, 0, j)),
        ],
        out_specs=pl.BlockSpec((2, rows, WIDE), lambda j: (0, 0, j)),
        compiler_params=params(),
        cost_estimate=cost(60 * rows * width, 12 * rows * width),
        name="light",
    )(phases, forward)


def launch_values(coef, terms, other, phase, fwd, launched):
    gradient = (coef[0] * terms[1].astype(F32) - coef[1] * terms[0].astype(F32)) + (
        coef[2] * other[1].astype(F32) - coef[3] * other[0].astype(F32)
    )
    updated = phase[0] - gradient
    sine, cosine = sincos(updated)
    f_re, f_im = fwd[0, 0].astype(F32), fwd[0, 1].astype(F32)
    launched[0] = (cosine * f_re - sine * f_im).astype(BF16)
    launched[1] = (sine * f_re + cosine * f_im).astype(BF16)
    return updated


def launch_kernel(coef, terms, other, phase, fwd, launched, phase_next):
    phase_next[0] = launch_values(coef, terms, other, phase, fwd, launched)


def launch(coef, terms, other, phases, forward):
    _, _, rows, width = forward.shape
    half = phases.shape[2] // WIDE
    tile = pl.BlockSpec((2, rows, WIDE), lambda j, c: (0, 0, j))
    plane = pl.BlockSpec((1, rows, WIDE), lambda j, c: (j // half, 0, j % half))
    return pl.pallas_call(
        launch_kernel,
        out_shape=(
            jax.ShapeDtypeStruct(forward.shape[1:], BF16),
            jax.ShapeDtypeStruct(phases.shape, F32),
        ),
        grid_spec=pltpu.PrefetchScalarGridSpec(
            num_scalar_prefetch=1,
            grid=(width // WIDE,),
            in_specs=[
                tile,
                tile,
                plane,
                pl.BlockSpec((1, 2, rows, WIDE), lambda j, c: (0, 0, 0, j)),
            ],
            out_specs=(tile, plane),
        ),
        compiler_params=params(),
        cost_estimate=cost(60 * rows * width, 24 * rows * width),
        name="launch",
    )(coef, terms, other, phases, forward)


def launch_edge_kernel(coef, terms, other, phase, fwd, launched):
    launch_values(coef, terms, other, phase, fwd, launched)


def launch_edges(coef, terms, other, phases, forward):
    _, _, rows, width = forward.shape
    wide = 2 * WIDE
    half = phases.shape[2] // wide
    far = rows // EDGE - 1
    tile = pl.BlockSpec((2, EDGE, wide), lambda e, j, c: (0, e * far, j))
    return pl.pallas_call(
        launch_edge_kernel,
        out_shape=jax.ShapeDtypeStruct((2, 2 * EDGE, width), BF16),
        grid_spec=pltpu.PrefetchScalarGridSpec(
            num_scalar_prefetch=1,
            grid=(2, width // wide),
            in_specs=[
                tile,
                tile,
                pl.BlockSpec((1, EDGE, wide), lambda e, j, c: (j // half, e * far, j % half)),
                pl.BlockSpec((1, 2, EDGE, wide), lambda e, j, c: (0, 0, e * far, j)),
            ],
            out_specs=pl.BlockSpec((2, EDGE, wide), lambda e, j, c: (0, e, j)),
        ),
        compiler_params=params(),
        cost_estimate=cost(120 * EDGE * width, 48 * EDGE * width),
        name="launch_edges",
    )(coef, terms, other, phases, forward)


def exchange_edges(first, last):
    tiles = lax.axis_size("tile")
    top = lax.ppermute(last, "tile", [(t, t + 1) for t in range(tiles - 1)])
    bottom = lax.ppermute(first, "tile", [(t + 1, t) for t in range(tiles - 1)])
    return top, bottom


def body(forward, adjoint_next, phase, blocks, offsets):
    block_total = offsets.shape[0]
    tiles = lax.axis_size("tile")
    modes = lax.axis_size("mode")
    mode = lax.axis_index("mode")
    rows, width = forward.shape[2], forward.shape[3]
    adjoint = adjoint_next[0]
    top, bottom = exchange_edges(adjoint[:, :EDGE], adjoint[:, rows - EDGE :])
    phases = lax.all_gather(phase, "mode", axis=0, tiled=False)

    raw_index = jnp.arange(block_total, dtype=jnp.int32)[:, None] + offsets
    inside = (raw_index >= 0) & (raw_index < block_total)
    pos = jnp.where(inside, offsets + RADIUS, -1).astype(jnp.int32)
    own_blocks = block_total // tiles
    start = lax.axis_index("tile") * own_blocks
    column_op = build(blocks, pos, WIDE // BLK, True)
    row_op = build(
        lax.dynamic_slice_in_dim(blocks, start, own_blocks, 1),
        lax.dynamic_slice_in_dim(pos, start, own_blocks, 0),
        min(WIDE // BLK, own_blocks),
        False,
    )

    back_middle = column_pass(adjoint, column_op, True)
    lit = light(phases, forward)
    terms, sums = adjoint_rows(top, bottom, column_op, back_middle, row_op, lit)
    other = lax.ppermute(terms, "mode", [(m, (m + 1) % modes) for m in range(modes)])
    own = jnp.sum(sums, axis=(1, 2))
    table = jnp.where(jnp.arange(modes)[:, None] == mode, own[None, :], 0.0)
    table = lax.psum(table, ("tile", "mode"))
    order = jnp.where(mode == 0, table, table[::-1])
    coef = order.reshape(-1) * (1.0 / (4.0 * width * modes))

    edges = launch_edges(coef, terms, other, phases, forward)
    edges = column_pass(edges, column_op, False)
    top, bottom = exchange_edges(edges[:, :EDGE], edges[:, EDGE:])
    launched, updated = launch(coef, terms, other, phases, forward)
    middle = column_pass(launched, column_op, False)
    phase_next = lax.dynamic_index_in_dim(updated, mode, 0, keepdims=False)
    return phase_next, forward_rows(top, middle, bottom, row_op)


def solution(mesh):
    placed = (
        P(("design", "mode"), None, "tile", None),
        P(("design", "mode"), None, "tile", None),
        P(("design", "tile"), "mode"),
        P(None, "design", None, None, None),
        P("design", None),
    )
    return jax.shard_map(
        body,
        mesh=mesh,
        in_specs=placed,
        out_specs=(P(("design", "tile"), "mode"), P(("design", "mode"), None, "tile", None)),
        check_vma=False,
    )
```

```python
import functools

import jax
import jax.numpy as jnp
from jax import lax
from jax.experimental import pallas as pl
from jax.experimental.pallas import tpu as pltpu
from jax.sharding import PartitionSpec as P

BLK = 64
RADIUS = 2
EDGE = RADIUS * BLK
WIDE = 256
VMEM_LIMIT = 56 * 1024 * 1024

F32 = jnp.float32
BF16 = jnp.bfloat16


def params():
    return pltpu.CompilerParams(vmem_limit_bytes=VMEM_LIMIT)


def cost(flops, moved):
    return pl.CostEstimate(flops=int(flops), bytes_accessed=int(moved), transcendentals=0)


def sincos(x):
    turns = jnp.round(x * 0.6366197723675814)
    r = x - turns * 1.5703125
    r = r - turns * 4.837512969970703125e-4
    r = r - turns * 7.549789954891882e-8
    quadrant = turns.astype(jnp.int32)
    z = r * r
    s = r + r * z * (-1.6666654611e-1 + z * (8.3321608736e-3 + z * -1.9515295891e-4))
    c = 1.0 - 0.5 * z + z * z * (4.166664568298827e-2 + z * (-1.388731625493765e-3 + z * 2.443315711809948e-5))
    swap = (quadrant & 1) == 1
    sine = jnp.where(swap, c, s)
    cosine = jnp.where(swap, s, c)
    sine = jnp.where((quadrant & 2) == 2, -sine, sine)
    cosine = jnp.where(((quadrant + 1) & 2) == 2, -cosine, cosine)
    return sine, cosine


def dot(a, b):
    return jnp.dot(a, b, preferred_element_type=F32)


def build_kernel(pos_ref, blk_ref, out_ref, *, group, transposed):
    base = pl.program_id(0) * group
    zero = jnp.zeros((BLK, BLK), F32)
    for part in range(2):
        strips = []
        for r in range(group):
            own = [blk_ref[part, r, k].astype(F32) for k in range(blk_ref.shape[2])]
            pieces = [zero] * r
            for d in range(2 * RADIUS + 1):
                piece = zero
                for k, block in enumerate(own):
                    piece = jnp.where(pos_ref[base + r, k] == d, block, piece)
                pieces.append(piece)
            pieces += [zero] * (group - 1 - r)
            strips.append(jnp.concatenate(pieces, axis=1))
        full = jnp.concatenate(strips, axis=0)
        if transposed:
            full = full.T
        out_ref[0, part] = full.astype(BF16)


def build(blocks, pos, group, transposed):
    _, rows, bands, _, _ = blocks.shape
    tall, wide = group * BLK, (group + 2 * RADIUS) * BLK
    if transposed:
        tall, wide = wide, tall
    count = rows // group
    return pl.pallas_call(
        functools.partial(build_kernel, group=group, transposed=transposed),
        out_shape=jax.ShapeDtypeStruct((count, 2, tall, wide), BF16),
        grid_spec=pltpu.PrefetchScalarGridSpec(
            num_scalar_prefetch=1,
            grid=(count,),
            in_specs=[pl.BlockSpec((2, group, bands, BLK, BLK), lambda g, p: (0, g, 0, 0, 0))],
            out_specs=pl.BlockSpec((1, 2, tall, wide), lambda g, p: (g, 0, 0, 0)),
        ),
        compiler_params=params(),
        cost_estimate=cost(0, 16 * rows * bands * BLK * BLK),
        name="build_operator",
    )(pos, blocks)


def window_specs(rows, groups):
    last = 2 * groups - 1
    return [
        pl.BlockSpec((2, rows, 128), lambda j: (0, 0, jnp.maximum(2 * j - 1, 0))),
        pl.BlockSpec((2, rows, WIDE), lambda j: (0, 0, j)),
        pl.BlockSpec((2, rows, 128), lambda j: (0, 0, jnp.minimum(2 * j + 2, last))),
    ]


def window(left, mid, right, part):
    return jnp.concatenate([left[part], mid[part], right[part]], axis=1)


def column_product(x_re, x_im, op_ref, conj):
    op_re, op_im = op_ref[0, 0], op_ref[0, 1]
    rr, ii = dot(x_re, op_re), dot(x_im, op_im)
    ri, ir = dot(x_re, op_im), dot(x_im, op_re)
    if conj:
        return (rr + ii).astype(BF16), (ri - ir).astype(BF16)
    return (rr - ii).astype(BF16), (ri + ir).astype(BF16)


def column_kernel(left, mid, right, op_ref, out_ref, *, conj):
    out_re, out_im = column_product(
        window(left, mid, right, 0), window(left, mid, right, 1), op_ref, conj
    )
    out_ref[0] = out_re
    out_ref[1] = out_im


def column_pass(field, op, conj):
    _, rows, width = field.shape
    groups = width // WIDE
    return pl.pallas_call(
        functools.partial(column_kernel, conj=conj),
        out_shape=jax.ShapeDtypeStruct(field.shape, BF16),
        grid=(groups,),
        in_specs=window_specs(rows, groups)
        + [pl.BlockSpec((1, 2, op.shape[2], WIDE), lambda j: (j, 0, 0, 0))],
        out_specs=pl.BlockSpec((2, rows, WIDE), lambda j: (0, 0, j)),
        compiler_params=params(),
        cost_estimate=cost(8 * rows * width * op.shape[2], 12 * rows * width + 2 * op.size),
        name="column_pass",
    )(field, field, field, op)


def row_groups(top, main, bottom, row_op):
    whole_re = jnp.concatenate([top[0], main[0], bottom[0]], axis=0)
    whole_im = jnp.concatenate([top[1], main[1], bottom[1]], axis=0)
    count, _, tall, deep = row_op.shape
    for i in range(count):
        m_re = whole_re[i * tall : i * tall + deep]
        m_im = whole_im[i * tall : i * tall + deep]
        op_re, op_im = row_op[i, 0], row_op[i, 1]
        out_re = dot(op_re, m_re) - dot(op_im, m_im)
        out_im = dot(op_re, m_im) + dot(op_im, m_re)
        yield i * tall, tall, out_re, out_im


def adjoint_row_kernel(tl, tm, tr, bl, bm, br, op_ref, main, row_op, lit, terms, sums):
    x_re = jnp.concatenate([window(tl, tm, tr, 0), window(bl, bm, br, 0)], axis=0)
    x_im = jnp.concatenate([window(tl, tm, tr, 1), window(bl, bm, br, 1)], axis=0)
    halo_re, halo_im = column_product(x_re, x_im, op_ref, True)

    @pl.when(pl.program_id(0) == 0)
    def _():
        sums[...] = jnp.zeros_like(sums)

    top = (halo_re[:EDGE], halo_im[:EDGE])
    bottom = (halo_re[EDGE:], halo_im[EDGE:])
    for low, tall, cj_re, cj_im in row_groups(top, main, bottom, row_op):
        cj_re = cj_re.astype(BF16).astype(F32)
        cj_im = cj_im.astype(BF16).astype(F32)
        lit_re = lit[0, low : low + tall].astype(F32)
        lit_im = lit[1, low : low + tall].astype(F32)
        t_re = cj_re * lit_re - cj_im * lit_im
        t_im = cj_re * lit_im + cj_im * lit_re
        terms[0, low : low + tall] = t_re.astype(BF16)
        terms[1, low : low + tall] = t_im.astype(BF16)
        sums[0] += jnp.sum(t_re.reshape(tall // 8, 8, WIDE), axis=0)
        sums[1] += jnp.sum(t_im.reshape(tall // 8, 8, WIDE), axis=0)


def adjoint_rows(top, bottom, op, main, row_op, lit):
    _, rows, width = main.shape
    groups = width // WIDE
    edge = window_specs(EDGE, groups)
    tile = pl.BlockSpec((2, rows, WIDE), lambda j: (0, 0, j))
    return pl.pallas_call(
        adjoint_row_kernel,
        out_shape=(
            jax.ShapeDtypeStruct(main.shape, BF16),
            jax.ShapeDtypeStruct((2, 8, WIDE), F32),
        ),
        grid=(groups,),
        in_specs=edge
        + edge
        + [
            pl.BlockSpec((1, 2, op.shape[2], WIDE), lambda j: (j, 0, 0, 0)),
            tile,
            pl.BlockSpec(row_op.shape, lambda j: (0, 0, 0, 0)),
            tile,
        ],
        out_specs=(tile, pl.BlockSpec((2, 8, WIDE), lambda j: (0, 0, 0))),
        compiler_params=params(),
        cost_estimate=cost(12 * rows * width * op.shape[2], 16 * rows * width),
        name="adjoint_rows",
    )(top, top, top, bottom, bottom, bottom, op, main, row_op, lit)


def forward_row_kernel(top, main, bottom, row_op, out):
    for low, tall, out_re, out_im in row_groups(top, main, bottom, row_op):
        out[0, 0, low : low + tall] = out_re.astype(BF16)
        out[0, 1, low : low + tall] = out_im.astype(BF16)


def forward_rows(top, main, bottom, row_op):
    _, rows, width = main.shape
    groups = width // WIDE
    edge = pl.BlockSpec((2, EDGE, WIDE), lambda j: (0, 0, j))
    return pl.pallas_call(
        forward_row_kernel,
        out_shape=jax.ShapeDtypeStruct((1,) + main.shape, BF16),
        grid=(groups,),
        in_specs=[
            edge,
            pl.BlockSpec((2, rows, WIDE), lambda j: (0, 0, j)),
            edge,
            pl.BlockSpec(row_op.shape, lambda j: (0, 0, 0, 0)),
        ],
        out_specs=pl.BlockSpec((1, 2, rows, WIDE), lambda j: (0, 0, 0, j)),
        compiler_params=params(),
        cost_estimate=cost(8 * rows * width * row_op.shape[3], 10 * rows * width),
        name="forward_rows",
    )(top, main, bottom, row_op)


def lit_kernel(phase, fwd, lit, first, last):
    sine, cosine = sincos(phase[0])
    f_re, f_im = fwd[0, 0].astype(F32), fwd[0, 1].astype(F32)
    for part, value in enumerate((cosine * f_re - sine * f_im, sine * f_re + cosine * f_im)):
        value = value.astype(BF16)
        lit[part] = value
        first[part] = value[:EDGE]
        last[part] = value[-EDGE:]


def light(phases, forward):
    _, _, rows, width = forward.shape
    half = phases.shape[2] // WIDE
    edge = jax.ShapeDtypeStruct((2, EDGE, width), BF16)
    return pl.pallas_call(
        lit_kernel,
        out_shape=(jax.ShapeDtypeStruct(forward.shape[1:], BF16), edge, edge),
        grid=(width // WIDE,),
        in_specs=[
            pl.BlockSpec((1, rows, WIDE), lambda j: (j // half, 0, j % half)),
            pl.BlockSpec((1, 2, rows, WIDE), lambda j: (0, 0, 0, j)),
        ],
        out_specs=(
            pl.BlockSpec((2, rows, WIDE), lambda j: (0, 0, j)),
            pl.BlockSpec((2, EDGE, WIDE), lambda j: (0, 0, j)),
            pl.BlockSpec((2, EDGE, WIDE), lambda j: (0, 0, j)),
        ),
        compiler_params=params(),
        cost_estimate=cost(60 * rows * width, 12 * rows * width),
        name="light",
    )(phases, forward)


def gradient_of(coef, terms, other):
    return (coef[0] * terms[1].astype(F32) - coef[1] * terms[0].astype(F32)) + (
        coef[2] * other[1].astype(F32) - coef[3] * other[0].astype(F32)
    )


def edge_gradient_kernel(coef, mode, t_top, t_bottom, o_top, o_bottom, first, last):
    first[...] = gradient_of(coef, t_top, o_top).astype(BF16)
    last[...] = gradient_of(coef, t_bottom, o_bottom).astype(BF16)


def edge_gradients(coef, mode, terms, other, columns):
    _, rows, _ = terms.shape
    wide = 2 * WIDE
    count = columns // wide
    far = rows // EDGE - 1
    top = pl.BlockSpec((2, EDGE, wide), lambda j, c, m: (0, 0, m[0] * count + j))
    bottom = pl.BlockSpec((2, EDGE, wide), lambda j, c, m: (0, far, m[0] * count + j))
    out = pl.BlockSpec((EDGE, wide), lambda j, c, m: (0, j))
    shape = jax.ShapeDtypeStruct((EDGE, columns), BF16)
    return pl.pallas_call(
        edge_gradient_kernel,
        out_shape=(shape, shape),
        grid_spec=pltpu.PrefetchScalarGridSpec(
            num_scalar_prefetch=2,
            grid=(count,),
            in_specs=[top, bottom, top, bottom],
            out_specs=(out, out),
        ),
        compiler_params=params(),
        cost_estimate=cost(20 * EDGE * columns, 20 * EDGE * columns),
        name="edge_gradients",
    )(coef, mode, terms, terms, other, other)


def ring_columns(ring, op_ref, out, step):
    left, mid, right = (step + 1) % 4, (step + 2) % 4, (step + 3) % 4

    def part(k):
        return jnp.concatenate(
            [ring[left, k, :, WIDE - EDGE :], ring[mid, k], ring[right, k, :, :EDGE]], axis=1
        )

    out_re, out_im = column_product(part(0), part(1), op_ref, False)
    out[0] = out_re
    out[1] = out_im


def launch_kernel(coef, mode, terms, other, phase, fwd, op_ref, out, phase_next, ring, *, groups, half):
    step = pl.program_id(0)

    @pl.when(step == 0)
    def _():
        ring[3] = jnp.zeros(ring.shape[1:], BF16)

    ring_columns(ring, op_ref, out, step)
    updated = phase[0] - gradient_of(coef, terms, other)
    sine, cosine = sincos(updated)
    f_re, f_im = fwd[0, 0].astype(F32), fwd[0, 1].astype(F32)
    ring[step % 4, 0] = (cosine * f_re - sine * f_im).astype(BF16)
    ring[step % 4, 1] = (sine * f_re + cosine * f_im).astype(BF16)
    keep = jnp.minimum(step, groups - 1) < (mode[0] + 1) * half
    phase_next[...] = jnp.where(keep, updated, phase_next[...])


def launch(coef, mode, terms, other, phases, forward, op):
    _, _, rows, width = forward.shape
    groups = width // WIDE
    half = phases.shape[2] // WIDE

    def chunk(j):
        return jnp.minimum(j, groups - 1)

    tile = pl.BlockSpec((2, rows, WIDE), lambda j, c, m: (0, 0, chunk(j)))
    return pl.pallas_call(
        functools.partial(launch_kernel, groups=groups, half=half),
        out_shape=(
            jax.ShapeDtypeStruct(forward.shape[1:], BF16),
            jax.ShapeDtypeStruct(phases.shape[1:], F32),
        ),
        grid_spec=pltpu.PrefetchScalarGridSpec(
            num_scalar_prefetch=2,
            grid=(groups + 2,),
            in_specs=[
                tile,
                tile,
                pl.BlockSpec((1, rows, WIDE), lambda j, c, m: (chunk(j) // half, 0, chunk(j) % half)),
                pl.BlockSpec((1, 2, rows, WIDE), lambda j, c, m: (0, 0, 0, chunk(j))),
                pl.BlockSpec((1, 2, op.shape[2], WIDE), lambda j, c, m: (jnp.maximum(j - 2, 0), 0, 0, 0)),
            ],
            out_specs=(
                pl.BlockSpec((2, rows, WIDE), lambda j, c, m: (0, 0, jnp.maximum(j - 2, 0))),
                pl.BlockSpec((rows, WIDE), lambda j, c, m: (0, jnp.clip(chunk(j) - m[0] * half, 0, half - 1))),
            ),
            scratch_shapes=[pltpu.VMEM((4, 2, rows, WIDE), BF16)],
        ),
        compiler_params=params(),
        cost_estimate=cost(8 * rows * width * op.shape[2], 24 * rows * width),
        name="launch",
    )(coef, mode, terms, other, phases, forward, op)


def turn_kernel(mode, lit_top, lit_bottom, own_top, own_bottom, far_top, far_bottom, op_ref, top, bottom, ring, *, groups, half):
    step = pl.program_id(0)

    @pl.when(step == 0)
    def _():
        ring[3] = jnp.zeros(ring.shape[1:], BF16)

    left, mid, right = (step + 1) % 4, (step + 2) % 4, (step + 3) % 4

    def part(k):
        return jnp.concatenate(
            [ring[left, k, :, WIDE - EDGE :], ring[mid, k], ring[right, k, :, :EDGE]], axis=1
        )

    out_re, out_im = column_product(part(0), part(1), op_ref, False)
    top[0] = out_re[:EDGE]
    top[1] = out_im[:EDGE]
    bottom[0] = out_re[EDGE:]
    bottom[1] = out_im[EDGE:]
    own_half = jnp.minimum(step, groups - 1) // half == mode[0]
    pairs = ((lit_top, own_top, far_top), (lit_bottom, own_bottom, far_bottom))
    for i, (lit, own, far) in enumerate(pairs):
        gradient = jnp.where(own_half, own[...].astype(F32), far[...].astype(F32))
        sine, cosine = sincos(gradient)
        l_re, l_im = lit[0].astype(F32), lit[1].astype(F32)
        ring[step % 4, 0, i * EDGE : (i + 1) * EDGE] = (cosine * l_re + sine * l_im).astype(BF16)
        ring[step % 4, 1, i * EDGE : (i + 1) * EDGE] = (cosine * l_im - sine * l_re).astype(BF16)


def turn_halos(mode, lit_halos, own, far, op):
    _, edge, width = lit_halos[0].shape
    groups = width // WIDE
    half = own[0].shape[1] // WIDE

    def chunk(j):
        return jnp.minimum(j, groups - 1)

    halo = pl.BlockSpec((2, edge, WIDE), lambda j, m: (0, 0, chunk(j)))
    grad = pl.BlockSpec((edge, WIDE), lambda j, m: (0, chunk(j) % half))
    out = pl.BlockSpec((2, edge, WIDE), lambda j, m: (0, 0, jnp.maximum(j - 2, 0)))
    shape = jax.ShapeDtypeStruct(lit_halos[0].shape, BF16)
    return pl.pallas_call(
        functools.partial(turn_kernel, groups=groups, half=half),
        out_shape=(shape, shape),
        grid_spec=pltpu.PrefetchScalarGridSpec(
            num_scalar_prefetch=1,
            grid=(groups + 2,),
            in_specs=[halo, halo, grad, grad, grad, grad]
            + [pl.BlockSpec((1, 2, op.shape[2], WIDE), lambda j, m: (jnp.maximum(j - 2, 0), 0, 0, 0))],
            out_specs=(out, out),
            scratch_shapes=[pltpu.VMEM((4, 2, 2 * edge, WIDE), BF16)],
        ),
        compiler_params=params(),
        cost_estimate=cost(16 * edge * width * op.shape[2], 24 * edge * width),
        name="turn_halos",
    )(mode, *lit_halos, *own, *far, op)


def exchange_edges(first, last):
    tiles = lax.axis_size("tile")
    top = lax.ppermute(last, "tile", [(t, t + 1) for t in range(tiles - 1)])
    bottom = lax.ppermute(first, "tile", [(t + 1, t) for t in range(tiles - 1)])
    return top, bottom


def body(forward, adjoint_next, phase, blocks, offsets):
    block_total = offsets.shape[0]
    tiles = lax.axis_size("tile")
    modes = lax.axis_size("mode")
    mode = lax.axis_index("mode")
    rows, width = forward.shape[2], forward.shape[3]
    adjoint = adjoint_next[0]
    top, bottom = exchange_edges(adjoint[:, :EDGE], adjoint[:, rows - EDGE :])
    phases = lax.all_gather(phase, "mode", axis=0, tiled=False)

    raw_index = jnp.arange(block_total, dtype=jnp.int32)[:, None] + offsets
    inside = (raw_index >= 0) & (raw_index < block_total)
    pos = jnp.where(inside, offsets + RADIUS, -1).astype(jnp.int32)
    own_blocks = block_total // tiles
    start = lax.axis_index("tile") * own_blocks
    column_op = build(blocks, pos, WIDE // BLK, True)
    row_op = build(
        lax.dynamic_slice_in_dim(blocks, start, own_blocks, 1),
        lax.dynamic_slice_in_dim(pos, start, own_blocks, 0),
        min(WIDE // BLK, own_blocks),
        False,
    )

    back_middle = column_pass(adjoint, column_op, True)
    lit, lit_first, lit_last = light(phases, forward)
    top, bottom, lit_first, lit_last = lax.optimization_barrier((top, bottom, lit_first, lit_last))
    lit_halos = exchange_edges(lit_first, lit_last)
    terms, sums = adjoint_rows(top, bottom, column_op, back_middle, row_op, lit)
    swap = [(m, (m + 1) % modes) for m in range(modes)]
    other = lax.ppermute(terms, "mode", swap)
    own = jnp.sum(sums, axis=(1, 2))
    table = jnp.where(jnp.arange(modes)[:, None] == mode, own[None, :], 0.0)
    table = lax.psum(table, ("tile", "mode"))
    order = jnp.where(mode == 0, table, table[::-1])
    coef = order.reshape(-1) * (1.0 / (4.0 * width * modes))

    where = mode.astype(jnp.int32).reshape(1)
    first, last = edge_gradients(coef, where, terms, other, phase.shape[1])
    own = exchange_edges(first, last)
    far = [lax.ppermute(half, "mode", swap) for half in own]
    middle, phase_next = launch(coef, where, terms, other, phases, forward, column_op)
    top, bottom = turn_halos(where, lit_halos, own, far, column_op)
    return phase_next, forward_rows(top, middle, bottom, row_op)


def solution(mesh):
    placed = (
        P(("design", "mode"), None, "tile", None),
        P(("design", "mode"), None, "tile", None),
        P(("design", "tile"), "mode"),
        P(None, "design", None, None, None),
        P("design", None),
    )
    return jax.shard_map(
        body,
        mesh=mesh,
        in_specs=placed,
        out_specs=(P(("design", "tile"), "mode"), P(("design", "mode"), None, "tile", None)),
        check_vma=False,
    )
```

```python
import functools

import jax
import jax.numpy as jnp
from jax import lax
from jax.experimental import pallas as pl
from jax.experimental.pallas import tpu as pltpu
from jax.sharding import PartitionSpec as P

BLK = 64
RADIUS = 2
EDGE = RADIUS * BLK
WIDE = 256
VMEM_LIMIT = 44 * 1024 * 1024

F32 = jnp.float32
BF16 = jnp.bfloat16


def params():
    return pltpu.CompilerParams(vmem_limit_bytes=VMEM_LIMIT)


def cost(flops, moved):
    return pl.CostEstimate(flops=int(flops), bytes_accessed=int(moved), transcendentals=0)


def sincos(x):
    turns = jnp.round(x * 0.6366197723675814)
    r = x - turns * 1.5703125
    r = r - turns * 4.837512969970703125e-4
    r = r - turns * 7.549789954891882e-8
    quadrant = turns.astype(jnp.int32)
    z = r * r
    s = r + r * z * (-1.6666654611e-1 + z * (8.3321608736e-3 + z * -1.9515295891e-4))
    c = 1.0 - 0.5 * z + z * z * (4.166664568298827e-2 + z * (-1.388731625493765e-3 + z * 2.443315711809948e-5))
    swap = (quadrant & 1) == 1
    sine = jnp.where(swap, c, s)
    cosine = jnp.where(swap, s, c)
    sine = jnp.where((quadrant & 2) == 2, -sine, sine)
    cosine = jnp.where(((quadrant + 1) & 2) == 2, -cosine, cosine)
    return sine, cosine


def dot(a, b):
    return jnp.dot(a, b, preferred_element_type=F32)


def build_kernel(pos_ref, blk_ref, out_ref, *, group, transposed):
    base = pl.program_id(0) * group
    zero = jnp.zeros((BLK, BLK), F32)
    for part in range(2):
        strips = []
        for r in range(group):
            own = [blk_ref[part, r, k].astype(F32) for k in range(blk_ref.shape[2])]
            pieces = [zero] * r
            for d in range(2 * RADIUS + 1):
                piece = zero
                for k, block in enumerate(own):
                    piece = jnp.where(pos_ref[base + r, k] == d, block, piece)
                pieces.append(piece)
            pieces += [zero] * (group - 1 - r)
            strips.append(jnp.concatenate(pieces, axis=1))
        full = jnp.concatenate(strips, axis=0)
        if transposed:
            full = full.T
        out_ref[0, part] = full.astype(BF16)


def build(blocks, pos, group, transposed):
    _, rows, bands, _, _ = blocks.shape
    tall, wide = group * BLK, (group + 2 * RADIUS) * BLK
    if transposed:
        tall, wide = wide, tall
    count = rows // group
    return pl.pallas_call(
        functools.partial(build_kernel, group=group, transposed=transposed),
        out_shape=jax.ShapeDtypeStruct((count, 2, tall, wide), BF16),
        grid_spec=pltpu.PrefetchScalarGridSpec(
            num_scalar_prefetch=1,
            grid=(count,),
            in_specs=[pl.BlockSpec((2, group, bands, BLK, BLK), lambda g, p: (0, g, 0, 0, 0))],
            out_specs=pl.BlockSpec((1, 2, tall, wide), lambda g, p: (g, 0, 0, 0)),
        ),
        compiler_params=params(),
        cost_estimate=cost(0, 16 * rows * bands * BLK * BLK),
        name="build_operator",
    )(pos, blocks)


def window_specs(rows, groups):
    last = 2 * groups - 1
    return [
        pl.BlockSpec((2, rows, 128), lambda j: (0, 0, jnp.maximum(2 * j - 1, 0))),
        pl.BlockSpec((2, rows, WIDE), lambda j: (0, 0, j)),
        pl.BlockSpec((2, rows, 128), lambda j: (0, 0, jnp.minimum(2 * j + 2, last))),
    ]


def window(left, mid, right, part):
    return jnp.concatenate([left[part], mid[part], right[part]], axis=1)


def column_product(x_re, x_im, op_ref, conj):
    op_re, op_im = op_ref[0, 0], op_ref[0, 1]
    rr, ii = dot(x_re, op_re), dot(x_im, op_im)
    ri, ir = dot(x_re, op_im), dot(x_im, op_re)
    if conj:
        return (rr + ii).astype(BF16), (ri - ir).astype(BF16)
    return (rr - ii).astype(BF16), (ri + ir).astype(BF16)


def column_kernel(left, mid, right, op_ref, out_ref, *, conj):
    out_re, out_im = column_product(
        window(left, mid, right, 0), window(left, mid, right, 1), op_ref, conj
    )
    out_ref[0] = out_re
    out_ref[1] = out_im


def column_pass(field, op, conj):
    _, rows, width = field.shape
    groups = width // WIDE
    return pl.pallas_call(
        functools.partial(column_kernel, conj=conj),
        out_shape=jax.ShapeDtypeStruct(field.shape, BF16),
        grid=(groups,),
        in_specs=window_specs(rows, groups)
        + [pl.BlockSpec((1, 2, op.shape[2], WIDE), lambda j: (j, 0, 0, 0))],
        out_specs=pl.BlockSpec((2, rows, WIDE), lambda j: (0, 0, j)),
        compiler_params=params(),
        cost_estimate=cost(8 * rows * width * op.shape[2], 12 * rows * width + 2 * op.size),
        name="column_pass",
    )(field, field, field, op)


def row_groups(top, main, bottom, row_op):
    whole_re = jnp.concatenate([top[0], main[0], bottom[0]], axis=0)
    whole_im = jnp.concatenate([top[1], main[1], bottom[1]], axis=0)
    count, _, tall, deep = row_op.shape
    for i in range(count):
        m_re = whole_re[i * tall : i * tall + deep]
        m_im = whole_im[i * tall : i * tall + deep]
        op_re, op_im = row_op[i, 0], row_op[i, 1]
        out_re = dot(op_re, m_re) - dot(op_im, m_im)
        out_im = dot(op_re, m_im) + dot(op_im, m_re)
        yield i * tall, tall, out_re, out_im


def adjoint_row_kernel(tl, tm, tr, bl, bm, br, op_ref, main, row_op, lit, terms, sums):
    x_re = jnp.concatenate([window(tl, tm, tr, 0), window(bl, bm, br, 0)], axis=0)
    x_im = jnp.concatenate([window(tl, tm, tr, 1), window(bl, bm, br, 1)], axis=0)
    halo_re, halo_im = column_product(x_re, x_im, op_ref, True)

    @pl.when(pl.program_id(0) == 0)
    def _():
        sums[...] = jnp.zeros_like(sums)

    top = (halo_re[:EDGE], halo_im[:EDGE])
    bottom = (halo_re[EDGE:], halo_im[EDGE:])
    for low, tall, cj_re, cj_im in row_groups(top, main, bottom, row_op):
        cj_re = cj_re.astype(BF16).astype(F32)
        cj_im = cj_im.astype(BF16).astype(F32)
        lit_re = lit[0, low : low + tall].astype(F32)
        lit_im = lit[1, low : low + tall].astype(F32)
        t_re = cj_re * lit_re - cj_im * lit_im
        t_im = cj_re * lit_im + cj_im * lit_re
        terms[0, low : low + tall] = t_re.astype(BF16)
        terms[1, low : low + tall] = t_im.astype(BF16)
        sums[0] += jnp.sum(t_re.reshape(tall // 8, 8, WIDE), axis=0)
        sums[1] += jnp.sum(t_im.reshape(tall // 8, 8, WIDE), axis=0)


def adjoint_rows(top, bottom, op, main, row_op, lit):
    _, rows, width = main.shape
    groups = width // WIDE
    edge = window_specs(EDGE, groups)
    tile = pl.BlockSpec((2, rows, WIDE), lambda j: (0, 0, j))
    return pl.pallas_call(
        adjoint_row_kernel,
        out_shape=(
            jax.ShapeDtypeStruct(main.shape, BF16),
            jax.ShapeDtypeStruct((2, 8, WIDE), F32),
        ),
        grid=(groups,),
        in_specs=edge
        + edge
        + [
            pl.BlockSpec((1, 2, op.shape[2], WIDE), lambda j: (j, 0, 0, 0)),
            tile,
            pl.BlockSpec(row_op.shape, lambda j: (0, 0, 0, 0)),
            tile,
        ],
        out_specs=(tile, pl.BlockSpec((2, 8, WIDE), lambda j: (0, 0, 0))),
        compiler_params=params(),
        cost_estimate=cost(12 * rows * width * op.shape[2], 16 * rows * width),
        name="adjoint_rows",
    )(top, top, top, bottom, bottom, bottom, op, main, row_op, lit)


def forward_row_kernel(top, main, bottom, row_op, out):
    for low, tall, out_re, out_im in row_groups(top, main, bottom, row_op):
        out[0, 0, low : low + tall] = out_re.astype(BF16)
        out[0, 1, low : low + tall] = out_im.astype(BF16)


def forward_rows(top, main, bottom, row_op):
    _, rows, width = main.shape
    groups = width // WIDE
    edge = pl.BlockSpec((2, EDGE, WIDE), lambda j: (0, 0, j))
    return pl.pallas_call(
        forward_row_kernel,
        out_shape=jax.ShapeDtypeStruct((1,) + main.shape, BF16),
        grid=(groups,),
        in_specs=[
            edge,
            pl.BlockSpec((2, rows, WIDE), lambda j: (0, 0, j)),
            edge,
            pl.BlockSpec(row_op.shape, lambda j: (0, 0, 0, 0)),
        ],
        out_specs=pl.BlockSpec((1, 2, rows, WIDE), lambda j: (0, 0, 0, j)),
        compiler_params=params(),
        cost_estimate=cost(8 * rows * width * row_op.shape[3], 10 * rows * width),
        name="forward_rows",
    )(top, main, bottom, row_op)


def lit_kernel(phase, fwd, lit):
    sine, cosine = sincos(phase[0])
    f_re, f_im = fwd[0, 0].astype(F32), fwd[0, 1].astype(F32)
    lit[0] = (cosine * f_re - sine * f_im).astype(BF16)
    lit[1] = (sine * f_re + cosine * f_im).astype(BF16)


def light(phases, forward):
    _, _, rows, width = forward.shape
    half = phases.shape[2] // WIDE
    return pl.pallas_call(
        lit_kernel,
        out_shape=jax.ShapeDtypeStruct(forward.shape[1:], BF16),
        grid=(width // WIDE,),
        in_specs=[
            pl.BlockSpec((1, rows, WIDE), lambda j: (j // half, 0, j % half)),
            pl.BlockSpec((1, 2, rows, WIDE), lambda j: (0, 0, 0, j)),
        ],
        out_specs=pl.BlockSpec((2, rows, WIDE), lambda j: (0, 0, j)),
        compiler_params=params(),
        cost_estimate=cost(60 * rows * width, 12 * rows * width),
        name="light",
    )(phases, forward)


def launch_values(coef, terms, other, phase, fwd, launched):
    gradient = (coef[0] * terms[1].astype(F32) - coef[1] * terms[0].astype(F32)) + (
        coef[2] * other[1].astype(F32) - coef[3] * other[0].astype(F32)
    )
    updated = phase[0] - gradient
    sine, cosine = sincos(updated)
    f_re, f_im = fwd[0, 0].astype(F32), fwd[0, 1].astype(F32)
    launched[0] = (cosine * f_re - sine * f_im).astype(BF16)
    launched[1] = (sine * f_re + cosine * f_im).astype(BF16)
    return updated


def launch_kernel(coef, terms, other, phase, fwd, launched, phase_next):
    phase_next[0] = launch_values(coef, terms, other, phase, fwd, launched)


def launch(coef, terms, other, phases, forward):
    _, _, rows, width = forward.shape
    half = phases.shape[2] // WIDE
    tile = pl.BlockSpec((2, rows, WIDE), lambda j, c: (0, 0, j))
    plane = pl.BlockSpec((1, rows, WIDE), lambda j, c: (j // half, 0, j % half))
    return pl.pallas_call(
        launch_kernel,
        out_shape=(
            jax.ShapeDtypeStruct(forward.shape[1:], BF16),
            jax.ShapeDtypeStruct(phases.shape, F32),
        ),
        grid_spec=pltpu.PrefetchScalarGridSpec(
            num_scalar_prefetch=1,
            grid=(width // WIDE,),
            in_specs=[
                tile,
                tile,
                plane,
                pl.BlockSpec((1, 2, rows, WIDE), lambda j, c: (0, 0, 0, j)),
            ],
            out_specs=(tile, plane),
        ),
        compiler_params=params(),
        cost_estimate=cost(60 * rows * width, 24 * rows * width),
        name="launch",
    )(coef, terms, other, phases, forward)


def launch_edge_kernel(coef, terms, other, phase, fwd, launched):
    launch_values(coef, terms, other, phase, fwd, launched)


def launch_edges(coef, terms, other, phases, forward):
    _, _, rows, width = forward.shape
    wide = 2 * WIDE
    half = phases.shape[2] // wide
    far = rows // EDGE - 1
    tile = pl.BlockSpec((2, EDGE, wide), lambda e, j, c: (0, e * far, j))
    return pl.pallas_call(
        launch_edge_kernel,
        out_shape=jax.ShapeDtypeStruct((2, 2 * EDGE, width), BF16),
        grid_spec=pltpu.PrefetchScalarGridSpec(
            num_scalar_prefetch=1,
            grid=(2, width // wide),
            in_specs=[
                tile,
                tile,
                pl.BlockSpec((1, EDGE, wide), lambda e, j, c: (j // half, e * far, j % half)),
                pl.BlockSpec((1, 2, EDGE, wide), lambda e, j, c: (0, 0, e * far, j)),
            ],
            out_specs=pl.BlockSpec((2, EDGE, wide), lambda e, j, c: (0, e, j)),
        ),
        compiler_params=params(),
        cost_estimate=cost(120 * EDGE * width, 48 * EDGE * width),
        name="launch_edges",
    )(coef, terms, other, phases, forward)


def complex_rows(op_re, op_im, m_re, m_im):
    return dot(op_re, m_re) - dot(op_im, m_im), dot(op_re, m_im) + dot(op_im, m_re)


def add_terms(cj_re, cj_im, lit_re, lit_im, terms, sums, low):
    tall = cj_re.shape[0]
    cj_re = cj_re.astype(BF16).astype(F32)
    cj_im = cj_im.astype(BF16).astype(F32)
    lit_re, lit_im = lit_re.astype(F32), lit_im.astype(F32)
    t_re = cj_re * lit_re - cj_im * lit_im
    t_im = cj_re * lit_im + cj_im * lit_re
    terms[0, low : low + tall] = t_re.astype(BF16)
    terms[1, low : low + tall] = t_im.astype(BF16)
    sums[0] += jnp.sum(t_re.reshape(tall // 8, 8, WIDE), axis=0)
    sums[1] += jnp.sum(t_im.reshape(tall // 8, 8, WIDE), axis=0)


def adjoint_inner_kernel(main, row_op, lit, terms, sums):
    @pl.when(pl.program_id(0) == 0)
    def _():
        sums[...] = jnp.zeros_like(sums)

    rows = main.shape[1]
    cj_re, cj_im = complex_rows(row_op[0, 0], row_op[0, 1], main[0], main[1])
    add_terms(cj_re, cj_im, lit[0, EDGE : rows - EDGE], lit[1, EDGE : rows - EDGE], terms, sums, 0)


def adjoint_inner(main, row_op, lit):
    _, rows, width = main.shape
    inner = rows - 2 * EDGE
    tile = pl.BlockSpec((2, rows, WIDE), lambda j: (0, 0, j))
    return pl.pallas_call(
        adjoint_inner_kernel,
        out_shape=(
            jax.ShapeDtypeStruct((2, inner, width), BF16),
            jax.ShapeDtypeStruct((2, 8, WIDE), F32),
        ),
        grid=(width // WIDE,),
        in_specs=[tile, pl.BlockSpec(row_op.shape, lambda j: (0, 0, 0, 0)), tile],
        out_specs=(
            pl.BlockSpec((2, inner, WIDE), lambda j: (0, 0, j)),
            pl.BlockSpec((2, 8, WIDE), lambda j: (0, 0, 0)),
        ),
        compiler_params=params(),
        cost_estimate=cost(8 * inner * width * rows, 12 * rows * width),
        name="adjoint_inner",
    )(main, row_op, lit)


def edge_windows(main, part, top, bottom):
    rows = main.shape[1]
    return (
        jnp.concatenate([top, main[part, : 2 * EDGE]], axis=0),
        jnp.concatenate([main[part, rows - 2 * EDGE :], bottom], axis=0),
    )


def adjoint_edge_kernel(tl, tm, tr, bl, bm, br, op_ref, main, edge_op, lit, before, terms, sums):
    x_re = jnp.concatenate([window(tl, tm, tr, 0), window(bl, bm, br, 0)], axis=0)
    x_im = jnp.concatenate([window(tl, tm, tr, 1), window(bl, bm, br, 1)], axis=0)
    halo_re, halo_im = column_product(x_re, x_im, op_ref, True)

    @pl.when(pl.program_id(0) == 0)
    def _():
        sums[...] = before[...]

    rows = main.shape[1]
    res = edge_windows(main, 0, halo_re[:EDGE], halo_re[EDGE:])
    ims = edge_windows(main, 1, halo_im[:EDGE], halo_im[EDGE:])
    for i, low in enumerate((0, rows - EDGE)):
        cj_re, cj_im = complex_rows(edge_op[i, 0], edge_op[i, 1], res[i], ims[i])
        add_terms(cj_re, cj_im, lit[0, low : low + EDGE], lit[1, low : low + EDGE], terms, sums, i * EDGE)


def adjoint_edges(top, bottom, op, main, edge_op, lit, before):
    _, rows, width = main.shape
    groups = width // WIDE
    edge = window_specs(EDGE, groups)
    tile = pl.BlockSpec((2, rows, WIDE), lambda j: (0, 0, j))
    return pl.pallas_call(
        adjoint_edge_kernel,
        out_shape=(
            jax.ShapeDtypeStruct((2, 2 * EDGE, width), BF16),
            jax.ShapeDtypeStruct((2, 8, WIDE), F32),
        ),
        grid=(groups,),
        in_specs=edge
        + edge
        + [
            pl.BlockSpec((1, 2, op.shape[2], WIDE), lambda j: (j, 0, 0, 0)),
            tile,
            pl.BlockSpec(edge_op.shape, lambda j: (0, 0, 0, 0)),
            tile,
            pl.BlockSpec((2, 8, WIDE), lambda j: (0, 0, 0)),
        ],
        out_specs=(
            pl.BlockSpec((2, 2 * EDGE, WIDE), lambda j: (0, 0, j)),
            pl.BlockSpec((2, 8, WIDE), lambda j: (0, 0, 0)),
        ),
        compiler_params=params(),
        cost_estimate=cost(32 * EDGE * width * op.shape[2], 16 * rows * width),
        name="adjoint_edges",
    )(top, top, top, bottom, bottom, bottom, op, main, edge_op, lit, before)


def forward_inner_kernel(main, row_op, out):
    out_re, out_im = complex_rows(row_op[0, 0], row_op[0, 1], main[0], main[1])
    out[0, 0] = out_re.astype(BF16)
    out[0, 1] = out_im.astype(BF16)


def forward_inner(main, row_op):
    _, rows, width = main.shape
    inner = rows // EDGE - 2
    deep = row_op.shape[3]
    return pl.pallas_call(
        forward_inner_kernel,
        out_shape=jax.ShapeDtypeStruct((1,) + main.shape, BF16),
        grid=(width // WIDE, inner),
        in_specs=[
            pl.BlockSpec((2, rows, WIDE), lambda j, i: (0, 0, j)),
            pl.BlockSpec((1, 2, EDGE, deep), lambda j, i: (0, 0, i, 0)),
        ],
        out_specs=pl.BlockSpec((1, 2, EDGE, WIDE), lambda j, i: (0, 0, i + 1, j)),
        compiler_params=params(),
        cost_estimate=cost(8 * inner * EDGE * width * rows, 8 * rows * width),
        name="forward_inner",
    )(main, row_op)


def forward_edge_kernel(top, main, bottom, edge_op, whole, out):
    side = pl.program_id(1)

    def run(m_re, m_im):
        out_re, out_im = complex_rows(edge_op[0, 0], edge_op[0, 1], m_re, m_im)
        out[0, 0] = out_re.astype(BF16)
        out[0, 1] = out_im.astype(BF16)

    @pl.when(side == 0)
    def _():
        run(*[jnp.concatenate([top[p], main[p]], axis=0) for p in range(2)])

    @pl.when(side == 1)
    def _():
        run(*[jnp.concatenate([main[p], bottom[p]], axis=0) for p in range(2)])


def forward_edges(top, main, bottom, edge_op, whole):
    _, rows, width = main.shape
    wide = 2 * WIDE
    near = rows // (2 * EDGE) - 1
    far = rows // EDGE - 1
    halo = pl.BlockSpec((2, EDGE, wide), lambda j, i: (0, 0, j))
    return pl.pallas_call(
        forward_edge_kernel,
        out_shape=jax.ShapeDtypeStruct(whole.shape, BF16),
        grid=(width // wide, 2),
        in_specs=[
            halo,
            pl.BlockSpec((2, 2 * EDGE, wide), lambda j, i: (0, i * near, j)),
            halo,
            pl.BlockSpec((1, 2, EDGE, edge_op.shape[3]), lambda j, i: (i, 0, 0, 0)),
            pl.BlockSpec(memory_space=pl.ANY),
        ],
        out_specs=pl.BlockSpec((1, 2, EDGE, wide), lambda j, i: (0, 0, i * far, j)),
        input_output_aliases={4: 0},
        compiler_params=params(),
        cost_estimate=cost(16 * EDGE * width * edge_op.shape[3], 24 * EDGE * width),
        name="forward_edges",
    )(top, main, bottom, edge_op, whole)


def gradient_of(coef, terms, other, rows):
    return (coef[0] * terms[1, rows].astype(F32) - coef[1] * terms[0, rows].astype(F32)) + (
        coef[2] * other[1, rows].astype(F32) - coef[3] * other[0, rows].astype(F32)
    )


def turned(phase, f_re, f_im):
    sine, cosine = sincos(phase)
    f_re, f_im = f_re.astype(F32), f_im.astype(F32)
    return (cosine * f_re - sine * f_im).astype(BF16), (sine * f_re + cosine * f_im).astype(BF16)


def ring_edge_kernel(coef, terms, other, p_top, p_bottom, f_top, f_bottom, op_ref, first, last, ring):
    step = pl.program_id(0)

    @pl.when(step == 0)
    def _():
        ring[3] = jnp.zeros(ring.shape[1:], BF16)

    left, mid, right = (step + 1) % 4, (step + 2) % 4, (step + 3) % 4

    def part(k):
        return jnp.concatenate(
            [ring[left, k, :, WIDE - EDGE :], ring[mid, k], ring[right, k, :, :EDGE]], axis=1
        )

    out_re, out_im = column_product(part(0), part(1), op_ref, False)
    first[0] = out_re[:EDGE]
    first[1] = out_im[:EDGE]
    last[0] = out_re[EDGE:]
    last[1] = out_im[EDGE:]
    for i, (phase, fwd) in enumerate(((p_top, f_top), (p_bottom, f_bottom))):
        span = slice(i * EDGE, (i + 1) * EDGE)
        updated = phase[0] - gradient_of(coef, terms, other, span)
        l_re, l_im = turned(updated, fwd[0, 0], fwd[0, 1])
        ring[step % 4, 0, span] = l_re
        ring[step % 4, 1, span] = l_im


def ring_edges(coef, terms, other, phases, forward, op):
    _, _, rows, width = forward.shape
    groups = width // WIDE
    half = phases.shape[2] // WIDE
    far = rows // EDGE - 1

    def chunk(j):
        return jnp.minimum(j, groups - 1)

    tile = pl.BlockSpec((2, 2 * EDGE, WIDE), lambda j, c: (0, 0, chunk(j)))
    out = pl.BlockSpec((2, EDGE, WIDE), lambda j, c: (0, 0, jnp.maximum(j - 2, 0)))
    shape = jax.ShapeDtypeStruct((2, EDGE, width), BF16)
    return pl.pallas_call(
        ring_edge_kernel,
        out_shape=(shape, shape),
        grid_spec=pltpu.PrefetchScalarGridSpec(
            num_scalar_prefetch=1,
            grid=(groups + 2,),
            in_specs=[
                tile,
                tile,
                pl.BlockSpec((1, EDGE, WIDE), lambda j, c: (chunk(j) // half, 0, chunk(j) % half)),
                pl.BlockSpec((1, EDGE, WIDE), lambda j, c: (chunk(j) // half, far, chunk(j) % half)),
                pl.BlockSpec((1, 2, EDGE, WIDE), lambda j, c: (0, 0, 0, chunk(j))),
                pl.BlockSpec((1, 2, EDGE, WIDE), lambda j, c: (0, 0, far, chunk(j))),
                pl.BlockSpec((1, 2, op.shape[2], WIDE), lambda j, c: (jnp.maximum(j - 2, 0), 0, 0, 0)),
            ],
            out_specs=(out, out),
            scratch_shapes=[pltpu.VMEM((4, 2, 2 * EDGE, WIDE), BF16)],
        ),
        compiler_params=params(),
        cost_estimate=cost(16 * EDGE * width * op.shape[2], 24 * EDGE * width),
        name="ring_edges",
    )(coef, terms, other, phases, phases, forward, forward, op)


def launch_split_kernel(coef, t_in, o_in, t_edge, o_edge, phase, fwd, launched, phase_next):
    rows = phase.shape[1]
    pieces = (
        (t_edge, o_edge, slice(0, EDGE), slice(0, EDGE)),
        (t_in, o_in, slice(0, rows - 2 * EDGE), slice(EDGE, rows - EDGE)),
        (t_edge, o_edge, slice(EDGE, 2 * EDGE), slice(rows - EDGE, rows)),
    )
    for terms, other, span, place in pieces:
        updated = phase[0, place] - gradient_of(coef, terms, other, span)
        phase_next[0, place] = updated
        l_re, l_im = turned(updated, fwd[0, 0, place], fwd[0, 1, place])
        launched[0, place] = l_re
        launched[1, place] = l_im


def launch_split(coef, t_in, o_in, t_edge, o_edge, phases, forward):
    _, _, rows, width = forward.shape
    half = phases.shape[2] // WIDE
    inner = pl.BlockSpec((2, rows - 2 * EDGE, WIDE), lambda j, c: (0, 0, j))
    edge = pl.BlockSpec((2, 2 * EDGE, WIDE), lambda j, c: (0, 0, j))
    plane = pl.BlockSpec((1, rows, WIDE), lambda j, c: (j // half, 0, j % half))
    return pl.pallas_call(
        launch_split_kernel,
        out_shape=(
            jax.ShapeDtypeStruct(forward.shape[1:], BF16),
            jax.ShapeDtypeStruct(phases.shape, F32),
        ),
        grid_spec=pltpu.PrefetchScalarGridSpec(
            num_scalar_prefetch=1,
            grid=(width // WIDE,),
            in_specs=[
                inner,
                inner,
                edge,
                edge,
                plane,
                pl.BlockSpec((1, 2, rows, WIDE), lambda j, c: (0, 0, 0, j)),
            ],
            out_specs=(pl.BlockSpec((2, rows, WIDE), lambda j, c: (0, 0, j)), plane),
        ),
        compiler_params=params(),
        cost_estimate=cost(60 * rows * width, 24 * rows * width),
        name="launch",
    )(coef, t_in, o_in, t_edge, o_edge, phases, forward)


def exchange_edges(first, last):
    tiles = lax.axis_size("tile")
    top = lax.ppermute(last, "tile", [(t, t + 1) for t in range(tiles - 1)])
    bottom = lax.ppermute(first, "tile", [(t + 1, t) for t in range(tiles - 1)])
    return top, bottom


def body(forward, adjoint_next, phase, blocks, offsets):
    block_total = offsets.shape[0]
    tiles = lax.axis_size("tile")
    modes = lax.axis_size("mode")
    mode = lax.axis_index("mode")
    rows, width = forward.shape[2], forward.shape[3]
    adjoint = adjoint_next[0]
    top, bottom = exchange_edges(adjoint[:, :EDGE], adjoint[:, rows - EDGE :])
    phases = lax.all_gather(phase, "mode", axis=0, tiled=False)

    raw_index = jnp.arange(block_total, dtype=jnp.int32)[:, None] + offsets
    inside = (raw_index >= 0) & (raw_index < block_total)
    pos = jnp.where(inside, offsets + RADIUS, -1).astype(jnp.int32)
    own_blocks = block_total // tiles
    split = own_blocks == 2 * RADIUS + WIDE // BLK
    start = lax.axis_index("tile") * own_blocks
    column_op = build(blocks, pos, WIDE // BLK, True)
    own_part = lax.dynamic_slice_in_dim(blocks, start, own_blocks, 1)
    own_pos = lax.dynamic_slice_in_dim(pos, start, own_blocks, 0)
    if split:
        inner = slice(RADIUS, own_blocks - RADIUS)
        row_op = build(own_part[:, inner], own_pos[inner], WIDE // BLK, False)
        ends = [own_part[:, :RADIUS], own_part[:, own_blocks - RADIUS :]]
        end_pos = [own_pos[:RADIUS], own_pos[own_blocks - RADIUS :]]
        edge_op = build(jnp.concatenate(ends, 1), jnp.concatenate(end_pos, 0), RADIUS, False)
    else:
        row_op = build(own_part, own_pos, min(WIDE // BLK, own_blocks), False)

    back_middle = column_pass(adjoint, column_op, True)
    lit = light(phases, forward)
    swap = [(m, (m + 1) % modes) for m in range(modes)]
    if split:
        t_in, s_in = adjoint_inner(back_middle, row_op, lit)
        o_in = lax.ppermute(t_in, "mode", swap)
        terms, sums = adjoint_edges(top, bottom, column_op, back_middle, edge_op, lit, s_in)
    else:
        terms, sums = adjoint_rows(top, bottom, column_op, back_middle, row_op, lit)
    other = lax.ppermute(terms, "mode", swap)
    own = jnp.sum(sums, axis=(1, 2))
    table = jnp.where(jnp.arange(modes)[:, None] == mode, own[None, :], 0.0)
    table = lax.psum(table, ("tile", "mode"))
    order = jnp.where(mode == 0, table, table[::-1])
    coef = order.reshape(-1) * (1.0 / (4.0 * width * modes))

    if split:
        first, last = ring_edges(coef, terms, other, phases, forward, column_op)
        top, bottom = exchange_edges(first, last)
        launched, updated = launch_split(coef, t_in, o_in, terms, other, phases, forward)
    else:
        edges = launch_edges(coef, terms, other, phases, forward)
        edges = column_pass(edges, column_op, False)
        top, bottom = exchange_edges(edges[:, :EDGE], edges[:, EDGE:])
        launched, updated = launch(coef, terms, other, phases, forward)
    middle = column_pass(launched, column_op, False)
    phase_next = lax.dynamic_index_in_dim(updated, mode, 0, keepdims=False)
    if split:
        whole = forward_inner(middle, row_op)
        return phase_next, forward_edges(top, middle, bottom, edge_op, whole)
    return phase_next, forward_rows(top, middle, bottom, row_op)


def solution(mesh):
    placed = (
        P(("design", "mode"), None, "tile", None),
        P(("design", "mode"), None, "tile", None),
        P(("design", "tile"), "mode"),
        P(None, "design", None, None, None),
        P("design", None),
    )
    return jax.shard_map(
        body,
        mesh=mesh,
        in_specs=placed,
        out_specs=(P(("design", "tile"), "mode"), P(("design", "mode"), None, "tile", None)),
        check_vma=False,
    )
```
